128 devices in a mesh: seq: 32 (over x_hi, z, y), dp: 4 (over x_lo, core).
Axes of the slice: x: 4 (x_hi: 2, x_lo: 2; x = x_hi * 2 + x_lo), y: 4, z: 4, core: 2. Of those that a mesh axis runs over, the one named last changes fastest.
Arguments:
- query_proj: bfloat16 [4, 2048, 4096], P('dp', None, 'seq'), may hold values from -6 to 6
- key_proj: bfloat16 [4, 2048, 4096], P('dp', None, 'seq'), may hold values from -6 to 6
- value_proj: bfloat16 [4, 2048, 4096], P('dp', None, 'seq'), may hold values from -6 to 6
- grad_out: bfloat16 [4, 2048, 4096], P('dp', None, 'seq'), may hold values from -6 to 6
- mode_gain: float32 [2048, 16], P('seq'), may hold values from -3 to 3
- decay_rate: float32 [2048, 16], P('seq'), may hold values from 0.5 to 128
- skip_gain: float32 [2048], P('seq'), may hold values from -4 to 4
Outputs:
- grad_query: bfloat16 [4, 2048, 4096], P('dp', None, 'seq')
- grad_key: bfloat16 [4, 2048, 4096], P('dp', None, 'seq')
- grad_value: bfloat16 [4, 2048, 4096], P('dp', None, 'seq')
- grad_modes: float32 [2048, 16], P('seq')
- grad_rate: float32 [2048, 16], P('seq')
- grad_skip: float32 [2048], P('seq')
The draws below stay inside these ranges and needn't reach their ends.
All inputs are finite; a program needn't handle non-finite values.
Results may differ from the reference program's by a relative error of at most 0.0095.
Values may be sent and summed in bfloat16 or wider, within the bound.
No kernel may reach another device: no remote copies, remote signals or barrier semaphores. Data moves between devices by JAX's collectives and lax.ppermute only.
A program may use at most 128 MiB of HBM per device.

```python
import math
import jax
import jax.numpy as jnp
from jax import lax

CH = 2048
MODES = 16
LEN = 4096
BATCH = 4


def block_scale(key, shape, shards, low, largest):
    def one(axis_at, blocks):
        draws = jax.random.uniform(jax.random.fold_in(jax.random.fold_in(key, 6), axis_at), (blocks,), jnp.float32, low / len(shards), largest / len(shards))
        return jnp.repeat(jnp.exp(draws), shape[axis_at] // blocks).reshape((-1,) + (1,) * (len(shape) - axis_at - 1))

    loudness = one(*shards[0])
    for cut in shards[1:]:
        loudness = loudness * one(*cut)
    return loudness


def normal_values(rng, shape, width, most, shards=(), kind=jnp.bfloat16):
    drawn = jax.random.normal(rng, shape, jnp.float32) * width
    if len(shards) > 0:
        drawn = block_scale(rng, shape, shards, -0.22, 0.18) * drawn
    return jnp.clip(drawn, min=-most, max=most).astype(kind)


def setup_inputs(seed: int = 0) -> dict:
    keys = jax.random.split(jax.random.key(seed), 8)
    return {
        "query_proj": normal_values(keys[0], (BATCH, CH, LEN), 1.0, 6.0, ((0, 4), (2, 32))),
        "key_proj": normal_values(keys[1], (BATCH, CH, LEN), 1.0, 6.0, ((0, 4), (2, 32))),
        "value_proj": normal_values(keys[2], (BATCH, CH, LEN), 1.0, 6.0, ((0, 4), (2, 32))),
        "grad_out": normal_values(keys[3], (BATCH, CH, LEN), 1.0, 6.0, ((0, 4), (2, 32))),
        "mode_gain": normal_values(keys[4], (CH, MODES), (MODES // 4) ** -0.5, 3.0, ((0, 32),), jnp.float32),
        "decay_rate": jnp.clip(jnp.exp(math.log(128.0) - 5.5451774 * jax.random.uniform(keys[5], (CH, MODES), jnp.float32) ** block_scale(keys[5], (CH, MODES), ((0, 32),), -0.2, 0.2)), 0.5, 128.0),
        "skip_gain": normal_values(keys[6], (CH,), 1.0, 4.0, ((0, 32),), jnp.float32),
    }


def reference(query_proj, key_proj, value_proj, grad_out, mode_gain, decay_rate, skip_gain):
    length = LEN
    padded_len = 2 * length
    positions = jnp.arange(length, dtype=jnp.float32) / length
    kernel = jnp.zeros((CH, length), jnp.float32)
    for which in range(MODES):
        kernel = kernel + mode_gain[:, which:which + 1] * jnp.exp(-decay_rate[:, which:which + 1] * positions[None, :])
    kernel = kernel / math.sqrt(length)
    spec_kernel = jnp.fft.rfft(kernel, n=padded_len, axis=-1)

    def one_sequence(carry, inputs):
        query_one, key_one, value_one, grad_one = inputs
        product = (key_one.astype(jnp.float32) * value_one.astype(jnp.float32)).astype(jnp.bfloat16)
        grad_mix = (grad_one.astype(jnp.float32) * query_one.astype(jnp.float32)).astype(jnp.bfloat16)
        prod_f = product.astype(jnp.float32)
        gmix_f = grad_mix.astype(jnp.float32)
        spec_prod = jnp.fft.rfft(prod_f, n=padded_len, axis=-1)
        spec_gmix = jnp.fft.rfft(gmix_f, n=padded_len, axis=-1)
        conv = jnp.fft.irfft(spec_kernel * spec_prod, n=padded_len, axis=-1)[:, :length]
        mixed = (conv + skip_gain[:, None] * prod_f).astype(jnp.bfloat16)
        corr = jnp.fft.irfft(jnp.conj(spec_kernel) * spec_gmix, n=padded_len, axis=-1)[:, :length]
        grad_prod = (corr + skip_gain[:, None] * gmix_f).astype(jnp.bfloat16)
        lags = jnp.fft.irfft(spec_gmix * jnp.conj(spec_prod), n=padded_len, axis=-1)[:, :length]
        grad_query = (grad_one.astype(jnp.float32) * mixed.astype(jnp.float32)).astype(jnp.bfloat16)
        grad_key = (grad_prod.astype(jnp.float32) * value_one.astype(jnp.float32)).astype(jnp.bfloat16)
        grad_value = (grad_prod.astype(jnp.float32) * key_one.astype(jnp.float32)).astype(jnp.bfloat16)
        carry = (carry[0] + lags.astype(jnp.float32), carry[1] + lax.optimization_barrier(jnp.sum(gmix_f * prod_f, axis=1)))
        return (carry, (grad_query, grad_key, grad_value))
    init = (jnp.zeros((CH, length), jnp.float32), jnp.zeros((CH,), jnp.float32))
    totals, grads = lax.scan(one_sequence, init, (query_proj, key_proj, value_proj, grad_out))
    lag_grad, skip_total = totals
    scale = 1.0 / math.sqrt(BATCH * length)
    mode_cols = []
    rate_cols = []
    for which in range(MODES):
        decay = jnp.exp(-decay_rate[:, which:which + 1] * positions[None, :])
        mode_cols.append(lax.optimization_barrier(jnp.sum(lag_grad * decay, axis=1)))
        rate_cols.append(-mode_gain[:, which] * lax.optimization_barrier(jnp.sum(lag_grad * positions[None, :] * decay, axis=1)))
    grad_modes = jnp.stack(mode_cols, axis=1) * (scale / math.sqrt(length))
    grad_rate = jnp.stack(rate_cols, axis=1) * (scale / math.sqrt(length))
    grad_skip = skip_total * scale
    return (grads[0], grads[1], grads[2], grad_modes, grad_rate, grad_skip)
```

```python
import functools
import math

import jax
import jax.numpy as jnp
from jax import lax
from jax.experimental import pallas as pl
from jax.experimental.pallas import tpu as pltpu
from jax.sharding import PartitionSpec as P

F32 = jnp.float32
BF16 = jnp.bfloat16


def split(x):
    head = x.astype(BF16)
    return head, (x - head.astype(F32)).astype(BF16)


def stack_split(x):
    return jnp.concatenate(split(x), axis=0)


def mm(a, b):
    return lax.dot_general(a, b, (((1,), (0,)), ((), ())), preferred_element_type=F32)


def mm3(x, table):
    rows = table.shape[0] // 2
    head, rest = split(x)
    return mm(head, table[:rows]) + mm(rest, table[:rows]) + mm(head, table[rows:])


def twice(x):
    return jnp.concatenate([x, x], axis=1)


def tables_kernel(
    span, length, modes, dcol_ref, gcol_ref, drow_ref, tp_ref, tg_ref, wp_ref, wg_ref, cy_ref, cx_ref, q_ref
):
    group = tp_ref.shape[0]
    lane = lax.broadcasted_iota(jnp.int32, (span, span), 1)
    row = lax.broadcasted_iota(jnp.int32, (span, span), 0)
    up = lane.astype(F32) / length
    down = (span - lane).astype(F32) / length
    dcol = dcol_ref[...]
    gain = gcol_ref[...] / math.sqrt(length)
    tab_y = gain * jnp.exp(-dcol * up)
    tab_x = gain * jnp.exp(-dcol * down)
    cy_ref[0] = stack_split(tab_y)
    cx_ref[0] = stack_split(tab_x)
    for c in range(group):
        tap_y = jnp.sum(tab_y[c * modes : (c + 1) * modes], axis=0, keepdims=True)
        tap_x = jnp.sum(tab_x[c * modes : (c + 1) * modes], axis=0, keepdims=True)
        wide_y = jnp.broadcast_to(tap_y, (span, span))
        wide_x = jnp.broadcast_to(tap_x, (span, span))
        toe_y = pltpu.roll(wide_y, 0, 1, stride=1, stride_axis=0)
        toe_x = pltpu.roll(wide_x, 0, 1, stride=1, stride_axis=0)
        tp_ref[c] = stack_split(jnp.where(lane > row, toe_y, 0.0))
        tg_ref[c] = stack_split(jnp.where(lane < row, toe_x, 0.0))
    drow = drow_ref[0]
    down_r = (span - row).astype(F32) / length
    up_r = row.astype(F32) / length
    wp = jnp.exp(-drow * down_r)
    wg = jnp.exp(-drow * up_r)
    wp_ref[0, 0] = stack_split(wp)
    wp_ref[0, 1] = stack_split(wp * down_r)
    wg_ref[0, 0] = stack_split(wg)
    wg_ref[0, 1] = stack_split(wg * up_r)
    step = lax.broadcasted_iota(jnp.int32, (8, span), 0)
    power = lax.shift_left(jnp.ones_like(step), step).astype(F32) * (span / length)
    q_ref[0] = jnp.exp(-drow * power)


def gather_channels(src, scratch, group, chunks):
    scratch[...] = src.astype(F32).reshape(chunks * group, src.shape[-1])
    return [scratch[pl.ds(c, chunks, stride=group), :] for c in range(group)]


def channel_masks(group, modes, chunks, span):
    owner = lax.broadcasted_iota(jnp.int32, (chunks, span), 1) // modes
    return [owner == c for c in range(group)]


def keep_own(full, masks, chunks):
    out = jnp.zeros((chunks, full.shape[1]), F32)
    for c, mask in enumerate(masks):
        out = jnp.where(mask, full[c * chunks : (c + 1) * chunks], out)
    return out


def scan_forward(x, q):
    rows = x.shape[0]
    index = lax.broadcasted_iota(jnp.int32, x.shape, 0)
    for j in range(rows.bit_length() - 1):
        hop = 1 << j
        x = x + q[j : j + 1] * jnp.where(index >= hop, pltpu.roll(x, hop, 0), 0.0)
    return jnp.where(index >= 1, pltpu.roll(x, 1, 0), 0.0)


def scan_backward(x, q):
    rows = x.shape[0]
    index = lax.broadcasted_iota(jnp.int32, x.shape, 0)
    for j in range(rows.bit_length() - 1):
        hop = 1 << j
        x = x + q[j : j + 1] * jnp.where(index < rows - hop, pltpu.roll(x, rows - hop, 0), 0.0)
    return jnp.where(index < rows - 1, pltpu.roll(x, rows - 1, 0), 0.0)


def conv_kernel(
    modes, direct_ref, data_ref, tp_ref, tg_ref, wp_ref, wg_ref, cy_ref, cx_ref, q_ref,
    out_ref, state_ref, in_p, in_g, out_y, out_x
):
    chunks, _, group, span = data_ref.shape
    base = pl.program_id(0) * group
    prods = gather_channels(data_ref[:, 0], in_p, group, chunks)
    gmixs = gather_channels(data_ref[:, 1], in_g, group, chunks)
    prod_b = [twice(x.astype(BF16)) for x in prods]
    gmix_b = [twice(x.astype(BF16)) for x in gmixs]
    masks = channel_masks(group, modes, chunks, span)
    q = q_ref[0]
    left = keep_own(mm(jnp.concatenate(prod_b, axis=0), wp_ref[0, 0]), masks, chunks)
    right = keep_own(mm(jnp.concatenate(gmix_b, axis=0), wg_ref[0, 0]), masks, chunks)
    before = scan_forward(left, q)
    after = scan_backward(right, q)
    state_ref[0, 0] = before
    state_ref[0, 1] = right
    spread_y = jnp.concatenate([jnp.where(m, before, 0.0) for m in masks], axis=0)
    spread_x = jnp.concatenate([jnp.where(m, after, 0.0) for m in masks], axis=0)
    cross_y = mm3(spread_y, cy_ref[0])
    cross_x = mm3(spread_x, cx_ref[0])
    for c in range(group):
        direct = direct_ref[base + c]
        rows = slice(c * chunks, (c + 1) * chunks)
        y = mm(prod_b[c], tp_ref[c]) + cross_y[rows] + direct * prods[c]
        x = mm(gmix_b[c], tg_ref[c]) + cross_x[rows] + direct * gmixs[c]
        out_y[pl.ds(c, chunks, stride=group), :] = y
        out_x[pl.ds(c, chunks, stride=group), :] = x
    out_ref[:, 0] = out_y[...].reshape(chunks, group, span).astype(BF16)
    out_ref[:, 1] = out_x[...].reshape(chunks, group, span).astype(BF16)


def grads_kernel(modes, length, data_ref, state_ref, wp_ref, wg_ref, q_ref, out_ref, in_p, in_g):
    chunks, _, group, span = data_ref.shape
    prods = gather_channels(data_ref[:, 0], in_p, group, chunks)
    gmixs = gather_channels(data_ref[:, 1], in_g, group, chunks)
    prod_b = [x.astype(BF16) for x in prods]
    gmix_b = [x.astype(BF16) for x in gmixs]
    masks = channel_masks(group, modes, chunks, span)
    q = q_ref[0]
    before = state_ref[0, 0]
    right = state_ref[0, 1]
    aged = keep_own(mm(twice(jnp.concatenate(prod_b, axis=0)), wp_ref[0, 1]), masks, chunks)
    right_aged = keep_own(mm(twice(jnp.concatenate(gmix_b, axis=0)), wg_ref[0, 1]), masks, chunks)
    before_aged = scan_forward(aged + q[0:1] * before * (span / length), q)
    mode_sum = jnp.sum(right * before, axis=0, keepdims=True)
    rate_sum = jnp.sum(right_aged * before + right * before_aged, axis=0, keepdims=True)
    lane = lax.broadcasted_iota(jnp.int32, (span, span), 1)
    row = lax.broadcasted_iota(jnp.int32, (span, span), 0)
    mirror = jnp.where(lane + row == span - 1, 1.0, 0.0).astype(BF16)
    turned_b = mm(jnp.concatenate(prod_b, axis=0), mirror).astype(BF16)
    keep = lane <= row
    lag_rows = []
    for c in range(group):
        outer = lax.dot_general(
            turned_b[c * chunks : (c + 1) * chunks],
            gmix_b[c],
            (((0,), (0,)), ((), ())),
            preferred_element_type=F32,
        )
        turned = pltpu.roll(outer, 1, 1, stride=1, stride_axis=0)
        lag_rows.append(jnp.sum(jnp.where(keep, turned, 0.0), axis=0, keepdims=True))
    lags = jnp.concatenate(lag_rows, axis=0)
    owner = lax.broadcasted_iota(jnp.int32, (group, span), 1) // modes
    own = owner == lax.broadcasted_iota(jnp.int32, (group, span), 0)

    def pick(full):
        return jnp.sum(jnp.where(own, full, 0.0), axis=0, keepdims=True)

    mode_sum = mode_sum + pick(mm3(lags, wg_ref[0, 0]))
    rate_sum = rate_sum + pick(mm3(lags, wg_ref[0, 1]))
    skip_sum = pick(jnp.broadcast_to(lags[:, 0:1], lags.shape))
    out_ref[0, 0:1] = mode_sum
    out_ref[0, 1:2] = rate_sum
    out_ref[0, 2:3] = skip_sum
    out_ref[0, 3:8] = jnp.zeros((5, span), F32)


def whole_block(*shape):
    zeros = (0,) * (len(shape) - 1)
    return pl.BlockSpec(shape, lambda i: (i,) + zeros)


def build(parts, channels, span, modes, length):
    group = span // modes
    steps = channels // group
    double = 2 * span

    def tables(decay, gain):
        return pl.pallas_call(
            functools.partial(tables_kernel, span, length, modes),
            grid=(steps,),
            in_specs=[whole_block(span, 1), whole_block(span, 1), whole_block(1, 1, span)],
            out_specs=[
                whole_block(group, double, span),
                whole_block(group, double, span),
                whole_block(1, 2, double, span),
                whole_block(1, 2, double, span),
                whole_block(1, double, span),
                whole_block(1, double, span),
                whole_block(1, 8, span),
            ],
            out_shape=[
                jax.ShapeDtypeStruct((channels, double, span), BF16),
                jax.ShapeDtypeStruct((channels, double, span), BF16),
                jax.ShapeDtypeStruct((steps, 2, double, span), BF16),
                jax.ShapeDtypeStruct((steps, 2, double, span), BF16),
                jax.ShapeDtypeStruct((steps, double, span), BF16),
                jax.ShapeDtypeStruct((steps, double, span), BF16),
                jax.ShapeDtypeStruct((steps, 8, span), F32),
            ],
            name="tables",
        )(decay.reshape(steps * span, 1), gain.reshape(steps * span, 1), decay.reshape(steps, 1, span))

    data_spec = pl.BlockSpec((parts, 2, group, span), lambda i: (0, 0, i, 0))

    def conv(direct, data, tp, tg, wp, wg, cy, cx, q):
        return pl.pallas_call(
            functools.partial(conv_kernel, modes),
            grid=(steps,),
            in_specs=[
                pl.BlockSpec(memory_space=pltpu.SMEM),
                data_spec,
                whole_block(group, double, span),
                whole_block(group, double, span),
                whole_block(1, 1, double, span),
                whole_block(1, 1, double, span),
                whole_block(1, double, span),
                whole_block(1, double, span),
                whole_block(1, 8, span),
            ],
            out_specs=[data_spec, whole_block(1, 2, parts, span)],
            out_shape=[
                jax.ShapeDtypeStruct(data.shape, BF16),
                jax.ShapeDtypeStruct((steps, 2, parts, span), F32),
            ],
            scratch_shapes=[pltpu.VMEM((parts * group, span), F32)] * 4,
            name="conv",
        )(direct, data, tp, tg, wp, wg, cy, cx, q)

    def grads(data, states, wp, wg, q):
        return pl.pallas_call(
            functools.partial(grads_kernel, modes, length),
            grid=(steps,),
            in_specs=[
                data_spec,
                whole_block(1, 2, parts, span),
                whole_block(1, 2, double, span),
                whole_block(1, 2, double, span),
                whole_block(1, 8, span),
            ],
            out_specs=whole_block(1, 8, span),
            out_shape=jax.ShapeDtypeStruct((steps, 8, span), F32),
            scratch_shapes=[pltpu.VMEM((parts * group, span), F32)] * 2,
            name="grads",
        )(data, states, wp, wg, q)

    return tables, conv, grads


def times(a, b):
    return (a.astype(F32) * b.astype(F32)).astype(BF16)


def body(query_proj, key_proj, value_proj, grad_out, mode_gain, decay_rate, skip_gain):
    _, all_channels, span = query_proj.shape
    parts = lax.axis_size("seq")
    batch = lax.axis_size("dp")
    channels, modes = mode_gain.shape
    length = parts * span
    query, key, value, grad = query_proj[0], key_proj[0], value_proj[0], grad_out[0]
    product = times(key, value).reshape(parts, channels, span)
    grad_mix = times(grad, query).reshape(parts, channels, span)
    sent = jnp.stack([product, grad_mix], axis=1)
    data = lax.all_to_all(sent, "seq", split_axis=0, concat_axis=0, tiled=True)

    tables, conv, grads = build(parts, channels, span, modes, length)
    direct = skip_gain + jnp.sum(mode_gain, axis=1) / math.sqrt(length)
    tp, tg, wp, wg, cy, cx, q = tables(decay_rate, mode_gain)
    outs, states = conv(direct, data, tp, tg, wp, wg, cy, cx, q)
    back = lax.all_to_all(outs, "seq", split_axis=0, concat_axis=0, tiled=True)
    sums = lax.psum(grads(data, states, wp, wg, q), "dp")

    mixed = back[:, 0].reshape(all_channels, span)
    grad_prod = back[:, 1].reshape(all_channels, span)
    grad_query = times(grad, mixed)[None]
    grad_key = times(grad_prod, value)[None]
    grad_value = times(grad_prod, key)[None]
    scale = 1.0 / math.sqrt(batch * length)
    grad_modes = sums[:, 0].reshape(channels, modes) * (scale / math.sqrt(length))
    grad_rate = -mode_gain * sums[:, 1].reshape(channels, modes) * (scale / math.sqrt(length))
    grad_skip = sums[:, 2].reshape(channels, modes)[:, 0] * scale
    return (grad_query, grad_key, grad_value, grad_modes, grad_rate, grad_skip)


def solution(mesh):
    acts = P("dp", None, "seq")
    return jax.shard_map(
        body,
        mesh=mesh,
        in_specs=(acts, acts, acts, acts, P("seq", None), P("seq", None), P("seq")),
        out_specs=(acts, acts, acts, P("seq", None), P("seq", None), P("seq")),
        check_vma=False,
    )
```

```python
import functools
import math

import jax
import jax.numpy as jnp
from jax import lax
from jax.experimental import pallas as pl
from jax.experimental.pallas import tpu as pltpu
from jax.sharding import PartitionSpec as P

F32 = jnp.float32
BF16 = jnp.bfloat16


def split(x):
    head = x.astype(BF16)
    return head, (x - head.astype(F32)).astype(BF16)


def stack_split(x):
    return jnp.concatenate(split(x), axis=0)


def mm(a, b):
    return lax.dot_general(a, b, (((1,), (0,)), ((), ())), preferred_element_type=F32)


def mm3(x, table):
    rows = table.shape[0] // 2
    head, rest = split(x)
    return mm(head, table[:rows]) + mm(rest, table[:rows]) + mm(head, table[rows:])


def twice(x):
    return jnp.concatenate([x, x], axis=1)


def products_kernel(query_ref, key_ref, value_ref, grad_ref, out_ref):
    parts, _, channels, span = out_ref.shape

    def put(slot, a_ref, b_ref):
        out = a_ref[...].astype(F32) * b_ref[...].astype(F32)
        out_ref[:, slot] = out.astype(BF16).reshape(parts, channels, span)

    put(0, key_ref, value_ref)
    put(1, grad_ref, query_ref)


def tables_kernel(length, decay_ref, gain_ref, tp_ref, tg_ref, wp_ref, wg_ref, cy_ref, cx_ref, q_ref):
    modes, channels = decay_ref.shape
    per = cy_ref.shape[0]
    span = cy_ref.shape[2]
    group = span // modes
    lane = lax.broadcasted_iota(jnp.int32, (span, span), 1)
    row = lax.broadcasted_iota(jnp.int32, (span, span), 0)
    up = lane.astype(F32) / length
    down = (span - lane).astype(F32) / length
    up_r = row.astype(F32) / length
    down_r = (span - row).astype(F32) / length
    step = lax.broadcasted_iota(jnp.int32, (8, span), 0)
    power = lax.shift_left(jnp.ones_like(step), step).astype(F32) * (span / length)
    first = pl.program_id(0) * (per * group)
    pad = jnp.zeros((modes, span - channels), F32)

    def turned(ref):
        return pltpu.roll(jnp.concatenate([ref[...], pad], axis=1), span - first, 1)

    decay = turned(decay_ref)
    gain = turned(gain_ref) / math.sqrt(length)
    for u in range(per):
        picks = range(u * group, (u + 1) * group)
        dcol = jnp.concatenate([jnp.broadcast_to(decay[:, c : c + 1], (modes, span)) for c in picks], axis=0)
        gcol = jnp.concatenate([jnp.broadcast_to(gain[:, c : c + 1], (modes, span)) for c in picks], axis=0)
        tab_y = gcol * jnp.exp(-dcol * up)
        tab_x = gcol * jnp.exp(-dcol * down)
        cy_ref[u] = stack_split(tab_y)
        cx_ref[u] = stack_split(tab_x)
        for c in range(group):
            tap_y = jnp.sum(tab_y[c * modes : (c + 1) * modes], axis=0, keepdims=True)
            tap_x = jnp.sum(tab_x[c * modes : (c + 1) * modes], axis=0, keepdims=True)
            wide_y = jnp.broadcast_to(tap_y, (span, span))
            wide_x = jnp.broadcast_to(tap_x, (span, span))
            toe_y = pltpu.roll(wide_y, 0, 1, stride=1, stride_axis=0)
            toe_x = pltpu.roll(wide_x, 0, 1, stride=1, stride_axis=0)
            tp_ref[u * group + c] = stack_split(jnp.where(lane > row, toe_y, 0.0))
            tg_ref[u * group + c] = stack_split(jnp.where(lane < row, toe_x, 0.0))
        drow = jnp.sum(jnp.where(lane == row, dcol, 0.0), axis=0, keepdims=True)
        wp = jnp.exp(-drow * down_r)
        wg = jnp.exp(-drow * up_r)
        wp_ref[u, 0] = stack_split(wp)
        wp_ref[u, 1] = stack_split(wp * down_r)
        wg_ref[u, 0] = stack_split(wg)
        wg_ref[u, 1] = stack_split(wg * up_r)
        q_ref[u] = jnp.exp(-drow * power)


def gather_channels(data_ref, slot, first, scratch, group):
    chunks, _, _, span = data_ref.shape
    picked = data_ref[:, slot, pl.ds(pl.multiple_of(first, group), group), :]
    scratch[...] = picked.astype(F32).reshape(chunks * group, span)
    return [scratch[pl.ds(c, chunks, stride=group), :] for c in range(group)]


def channel_masks(group, modes, chunks, span):
    owner = lax.broadcasted_iota(jnp.int32, (chunks, span), 1) // modes
    return [owner == c for c in range(group)]


def keep_own(full, masks, chunks):
    out = jnp.zeros((chunks, full.shape[1]), F32)
    for c, mask in enumerate(masks):
        out = jnp.where(mask, full[c * chunks : (c + 1) * chunks], out)
    return out


def scan_forward(x, q):
    rows = x.shape[0]
    index = lax.broadcasted_iota(jnp.int32, x.shape, 0)
    for j in range(rows.bit_length() - 1):
        hop = 1 << j
        x = x + q[j : j + 1] * jnp.where(index >= hop, pltpu.roll(x, hop, 0), 0.0)
    return jnp.where(index >= 1, pltpu.roll(x, 1, 0), 0.0)


def scan_backward(x, q):
    rows = x.shape[0]
    index = lax.broadcasted_iota(jnp.int32, x.shape, 0)
    for j in range(rows.bit_length() - 1):
        hop = 1 << j
        x = x + q[j : j + 1] * jnp.where(index < rows - hop, pltpu.roll(x, rows - hop, 0), 0.0)
    return jnp.where(index < rows - 1, pltpu.roll(x, rows - 1, 0), 0.0)


def conv_kernel(
    modes, direct_ref, data_ref, tp_ref, tg_ref, wp_ref, wg_ref, cy_ref, cx_ref, q_ref,
    out_ref, state_ref, in_p, in_g, out_y, out_x
):
    chunks, _, _, span = data_ref.shape
    per = q_ref.shape[0]
    group = span // modes
    base = pl.program_id(0) * (per * group)
    masks = channel_masks(group, modes, chunks, span)
    for u in range(per):
        first = base + u * group
        prods = gather_channels(data_ref, 0, first, in_p.at[u], group)
        gmixs = gather_channels(data_ref, 1, first, in_g.at[u], group)
        prod_b = [twice(x.astype(BF16)) for x in prods]
        gmix_b = [twice(x.astype(BF16)) for x in gmixs]
        q = q_ref[u]
        left = keep_own(mm(jnp.concatenate(prod_b, axis=0), wp_ref[u, 0]), masks, chunks)
        right = keep_own(mm(jnp.concatenate(gmix_b, axis=0), wg_ref[u, 0]), masks, chunks)
        before = scan_forward(left, q)
        after = scan_backward(right, q)
        state_ref[u, 0] = before
        state_ref[u, 1] = right
        spread_y = jnp.concatenate([jnp.where(m, before, 0.0) for m in masks], axis=0)
        spread_x = jnp.concatenate([jnp.where(m, after, 0.0) for m in masks], axis=0)
        cross_y = mm3(spread_y, cy_ref[u])
        cross_x = mm3(spread_x, cx_ref[u])
        for c in range(group):
            direct = direct_ref[first + c]
            rows = slice(c * chunks, (c + 1) * chunks)
            k = u * group + c
            y = mm(prod_b[c], tp_ref[k]) + cross_y[rows] + direct * prods[c]
            x = mm(gmix_b[c], tg_ref[k]) + cross_x[rows] + direct * gmixs[c]
            out_y[u, pl.ds(c, chunks, stride=group), :] = y
            out_x[u, pl.ds(c, chunks, stride=group), :] = x
        place = slice(u * group, (u + 1) * group)
        out_ref[:, 0, place] = out_y[u].reshape(chunks, group, span).astype(BF16)
        out_ref[:, 1, place] = out_x[u].reshape(chunks, group, span).astype(BF16)


def grads_kernel(modes, length, data_ref, state_ref, wp_ref, wg_ref, q_ref, out_ref, in_p, in_g, rows_ref):
    chunks, _, channels, span = data_ref.shape
    per = q_ref.shape[0]
    group = span // modes
    base = pl.program_id(0) * (per * group)
    masks = channel_masks(group, modes, chunks, span)
    lane = lax.broadcasted_iota(jnp.int32, (span, span), 1)
    row = lax.broadcasted_iota(jnp.int32, (span, span), 0)
    mirror = jnp.where(lane + row == span - 1, 1.0, 0.0).astype(BF16)
    keep = lane <= row
    owner = lax.broadcasted_iota(jnp.int32, (group, span), 1) // modes
    own = owner == lax.broadcasted_iota(jnp.int32, (group, span), 0)
    for u in range(per):
        first = base + u * group
        prods = gather_channels(data_ref, 0, first, in_p.at[u], group)
        gmixs = gather_channels(data_ref, 1, first, in_g.at[u], group)
        prod_b = jnp.concatenate([x.astype(BF16) for x in prods], axis=0)
        gmix_b = jnp.concatenate([x.astype(BF16) for x in gmixs], axis=0)
        q = q_ref[u]
        before = state_ref[u, 0]
        right = state_ref[u, 1]
        aged = keep_own(mm(twice(prod_b), wp_ref[u, 1]), masks, chunks)
        right_aged = keep_own(mm(twice(gmix_b), wg_ref[u, 1]), masks, chunks)
        before_aged = scan_forward(aged + q[0:1] * before * (span / length), q)
        mode_sum = jnp.sum(right * before, axis=0, keepdims=True)
        rate_sum = jnp.sum(right_aged * before + right * before_aged, axis=0, keepdims=True)
        turned_b = mm(prod_b, mirror).astype(BF16)
        lag_rows = []
        for c in range(group):
            rows = slice(c * chunks, (c + 1) * chunks)
            outer = lax.dot_general(
                turned_b[rows], gmix_b[rows], (((0,), (0,)), ((), ())), preferred_element_type=F32
            )
            turned = pltpu.roll(outer, 1, 1, stride=1, stride_axis=0)
            lag_rows.append(jnp.sum(jnp.where(keep, turned, 0.0), axis=0, keepdims=True))
        lags = jnp.concatenate(lag_rows, axis=0)
        place = pl.ds(pl.multiple_of(first, group), group)
        rows_ref[0, place, :] = jnp.where(own, mm3(lags, wg_ref[u, 0]) + mode_sum, 0.0)
        rows_ref[1, place, :] = jnp.where(own, mm3(lags, wg_ref[u, 1]) + rate_sum, 0.0)
        rows_ref[2, place, :] = jnp.where(own, lags[:, 0:1], 0.0)

    @pl.when(pl.program_id(0) == pl.num_programs(0) - 1)
    def _():
        mode = lax.broadcasted_iota(jnp.int32, (modes, span), 0)
        at = lax.broadcasted_iota(jnp.int32, (modes, span), 1)
        choose = jnp.where(lax.rem(at, modes) == mode, 1.0, 0.0)
        for k in range(3):
            out_ref[k] = lax.dot_general(
                choose,
                rows_ref[k],
                (((1,), (1,)), ((), ())),
                precision=lax.Precision.HIGHEST,
                preferred_element_type=F32,
            )


def whole_block(*shape):
    zeros = (0,) * (len(shape) - 1)
    return pl.BlockSpec(shape, lambda i: (i,) + zeros)


def build(parts, all_channels, channels, span, modes, length, per):
    group = span // modes
    steps = channels // group
    double = 2 * span
    whole = pl.BlockSpec(memory_space=pltpu.VMEM)

    def products(query, key, value, grad, cuts=4):
        rows = pl.BlockSpec((all_channels // cuts, span), lambda i: (i, 0))
        return pl.pallas_call(
            products_kernel,
            grid=(cuts,),
            in_specs=[rows] * 4,
            out_specs=whole_block(parts // cuts, 2, channels, span),
            out_shape=jax.ShapeDtypeStruct((parts, 2, channels, span), BF16),
            name="products",
        )(query, key, value, grad)

    def tables(decay, gain):
        return pl.pallas_call(
            functools.partial(tables_kernel, length),
            grid=(steps // per,),
            in_specs=[whole, whole],
            out_specs=[
                whole_block(per * group, double, span),
                whole_block(per * group, double, span),
                whole_block(per, 2, double, span),
                whole_block(per, 2, double, span),
                whole_block(per, double, span),
                whole_block(per, double, span),
                whole_block(per, 8, span),
            ],
            out_shape=[
                jax.ShapeDtypeStruct((channels, double, span), BF16),
                jax.ShapeDtypeStruct((channels, double, span), BF16),
                jax.ShapeDtypeStruct((steps, 2, double, span), BF16),
                jax.ShapeDtypeStruct((steps, 2, double, span), BF16),
                jax.ShapeDtypeStruct((steps, double, span), BF16),
                jax.ShapeDtypeStruct((steps, double, span), BF16),
                jax.ShapeDtypeStruct((steps, 8, span), F32),
            ],
            name="tables",
        )(decay, gain)

    def conv(direct, data, tp, tg, wp, wg, cy, cx, q):
        return pl.pallas_call(
            functools.partial(conv_kernel, modes),
            grid=(steps // per,),
            in_specs=[
                pl.BlockSpec(memory_space=pltpu.SMEM),
                whole,
                whole_block(per * group, double, span),
                whole_block(per * group, double, span),
                whole_block(per, 1, double, span),
                whole_block(per, 1, double, span),
                whole_block(per, double, span),
                whole_block(per, double, span),
                whole_block(per, 8, span),
            ],
            out_specs=[
                pl.BlockSpec((parts, 2, per * group, span), lambda i: (0, 0, i, 0)),
                whole_block(per, 2, parts, span),
            ],
            out_shape=[
                jax.ShapeDtypeStruct(data.shape, BF16),
                jax.ShapeDtypeStruct((steps, 2, parts, span), F32),
            ],
            scratch_shapes=[pltpu.VMEM((per, parts * group, span), F32)] * 4,
            name="conv",
        )(direct, data, tp, tg, wp, wg, cy, cx, q)

    def grads(data, states, wp, wg, q):
        return pl.pallas_call(
            functools.partial(grads_kernel, modes, length),
            grid=(steps // per,),
            in_specs=[
                whole,
                whole_block(per, 2, parts, span),
                whole_block(per, 2, double, span),
                whole_block(per, 2, double, span),
                whole_block(per, 8, span),
            ],
            out_specs=whole,
            out_shape=jax.ShapeDtypeStruct((3, modes, channels), F32),
            scratch_shapes=[pltpu.VMEM((per, parts * group, span), F32)] * 2
            + [pltpu.VMEM((3, channels, span), F32)],
            name="grads",
        )(data, states, wp, wg, q)

    return products, tables, conv, grads


def times(a, b):
    return (a.astype(F32) * b.astype(F32)).astype(BF16)


def exchange(x):
    return lax.all_to_all(x, "seq", split_axis=0, concat_axis=0, tiled=True)


def butterfly_sum(x, axis):
    size = lax.axis_size(axis)
    hop = 1
    while hop < size:
        x = x + lax.ppermute(x, axis, [(i, i ^ hop) for i in range(size)])
        hop *= 2
    return x


def body(query_proj, key_proj, value_proj, grad_out, mode_gain, decay_rate, skip_gain):
    _, all_channels, span = query_proj.shape
    parts = lax.axis_size("seq")
    batch = lax.axis_size("dp")
    channels, modes = mode_gain.shape
    length = parts * span
    query, key, value, grad = query_proj[0], key_proj[0], value_proj[0], grad_out[0]
    products, tables, conv, grads = build(parts, all_channels, channels, span, modes, length, 2)
    sent = products(query, key, value, grad)
    data = pltpu.with_memory_space_constraint(exchange(sent), pltpu.VMEM)

    direct = skip_gain + jnp.sum(mode_gain, axis=1) / math.sqrt(length)
    tp, tg, wp, wg, cy, cx, q = tables(decay_rate.T, mode_gain.T)
    outs, states = conv(direct, data, tp, tg, wp, wg, cy, cx, q)
    back = exchange(outs)
    sums = butterfly_sum(grads(data, states, wp, wg, q), "dp")

    mixed = back[:, 0].reshape(all_channels, span)
    grad_prod = back[:, 1].reshape(all_channels, span)
    grad_query = times(grad, mixed)[None]
    grad_key = times(grad_prod, value)[None]
    grad_value = times(grad_prod, key)[None]
    scale = 1.0 / math.sqrt(batch * length)
    grad_modes = (sums[0] * (scale / math.sqrt(length))).T
    grad_rate = (-mode_gain.T * sums[1] * (scale / math.sqrt(length))).T
    grad_skip = sums[2, 0] * scale
    return (grad_query, grad_key, grad_value, grad_modes, grad_rate, grad_skip)


def solution(mesh):
    acts = P("dp", None, "seq")
    return jax.shard_map(
        body,
        mesh=mesh,
        in_specs=(acts, acts, acts, acts, P("seq", None), P("seq", None), P("seq")),
        out_specs=(acts, acts, acts, P("seq", None), P("seq", None), P("seq")),
        check_vma=False,
    )
```
